128 devices in a mesh: dp: 4 (over x), seq: 16 (over y, z), mp: 2 (over core).
Axes of the slice: x: 4, y: 4, z: 4, core: 2. Of those that a mesh axis runs over, the one named last changes fastest.
Arguments:
- queries: bfloat16 [24576, 2048], P(('dp', 'seq'), 'mp'), may hold values from -64 to 64
- keys: bfloat16 [24576, 512], P(('dp', 'seq'), 'mp'), may hold values from -64 to 64
- values: bfloat16 [24576, 512], P(('dp', 'seq'), 'mp'), may hold values from -16 to 16
- offsets: int32 [24576], P(('dp', 'seq')), may hold values from 0 to 6143, as said below
- out_weight: bfloat16 [2048, 4096], P('mp'), may hold values from -0.125 to 0.125
- stream_in: bfloat16 [24576, 4096], P(('dp', 'seq'), 'mp'), may hold values from -64 to 64
- norm_gain: float32 [4096], replicated, may hold values from 0.1 to 1.9
- head_weight: bfloat16 [65536, 4096], P(('dp', 'seq', 'mp')), may hold values from -15 to 15
- picks: int32 [1024], P(('dp', 'seq')), may hold values from 0 to 383
- targets: int32 [1024], replicated, may hold values from 0 to 65535
Outputs:
- stream_out: bfloat16 [24576, 4096], P(('dp', 'seq'), 'mp')
- logprob: float32 [1024], P(('dp', 'seq', 'mp'))
The draws below stay inside these ranges and needn't reach their ends.
Inputs may be any that keep to these rules, and one draw needn't show every extreme that they name: Each pack is cut into two to four consecutive rollouts; offsets[t] is the first position of the rollout that holds t, so offsets[t] <= t % 6144, and t % 6144 - offsets[t] is at most 3071, reached in every pack.
All inputs are finite; a program needn't handle non-finite values.
Results may differ from the reference program's by a relative error of at most 0.013.
Values may be sent and summed in bfloat16 or wider, within the bound.
No kernel may reach another device: no remote copies, remote signals or barrier semaphores. Data moves between devices by JAX's collectives and lax.ppermute only.
A program may use at most 128 MiB of HBM per device.

```python
import math
import jax
import jax.numpy as jnp
from jax import lax

D = 4096
HD = 128
HEADS = 16
KV_HEADS = 4
TOK_DEV = 384
SC_DEV = 16
GROUP = 4
BATCH = 4
PACK = 6144
TOKENS = 24576
SCORED = 256
VOCAB = 65536
MAXLEN = 3072
QB = 384


def draw_queries(key, part):
    drawn = jax.random.normal(jax.random.fold_in(key, 11), (TOKENS, HEADS * HD), jnp.float32)
    return drawn.astype(jnp.bfloat16)


def draw_keys(key, part):
    drawn = jax.random.normal(jax.random.fold_in(key, 21), (TOKENS, KV_HEADS * HD), jnp.float32)
    return drawn.astype(jnp.bfloat16)


def draw_offsets(key, part):

    def one_pack(index):
        pack_key = jax.random.fold_in(key, index)
        spans = jax.random.randint(jax.random.fold_in(pack_key, 1), (PACK,), MAXLEN // 3, MAXLEN + 1)
        longest = jax.random.randint(jax.random.fold_in(pack_key, 2), (), 0, 2)
        spans = jnp.where(jnp.arange(PACK) == longest, MAXLEN, spans).astype(jnp.int32)
        ends = jnp.cumsum(spans)
        owner = jnp.searchsorted(ends, jnp.arange(PACK, dtype=jnp.int32), side='right')
        return (ends[owner] - spans[owner]).astype(jnp.int32)
    return jax.vmap(one_pack)(jnp.arange(BATCH, dtype=jnp.int32)).reshape(TOKENS)


def draw_stream_in(key, part):
    base = jax.random.normal(jax.random.fold_in(key, 31), (TOKENS, D), jnp.float32)
    rows = jnp.exp(jax.random.uniform(jax.random.fold_in(key, 32), (TOKENS, 1), jnp.float32, math.log(0.3), math.log(3.0)))
    cols = jnp.exp(jax.random.uniform(jax.random.fold_in(key, 33), (1, D), jnp.float32, math.log(0.5), math.log(2.0)))
    return (base * rows * cols).astype(jnp.bfloat16)


def draw_head_weight(key, part):
    width_scale = 3.0 / math.sqrt(D)
    drawn = jax.random.normal(jax.random.fold_in(key, 41), (VOCAB, D), jnp.float32) * width_scale
    return drawn.astype(jnp.bfloat16)


def plant(entries, rng, least, top_value):
    shape = entries.shape
    index_at = [jax.random.randint(jax.random.fold_in(rng, axis), (), 0, shape[axis]) for axis in range(len(shape))]
    entries = entries.at[tuple(index_at)].set(least)
    longest = shape.index(max(shape))
    index_at[longest] = (index_at[longest] + 1) % shape[longest]
    return entries.at[tuple(index_at)].set(top_value)


def block_scale(stream_key, extent, split, low, largest):
    def one(position, parts):
        draws = jax.random.uniform(jax.random.fold_in(jax.random.fold_in(stream_key, 6), position), (parts,), jnp.float32, low / len(split), largest / len(split))
        return jnp.repeat(jnp.exp(draws), extent[position] // parts).reshape((-1,) + (1,) * (len(extent) - position - 1))

    level = one(*split[0])
    for cut in split[1:]:
        level = level * one(*cut)
    return level


def noise(stream_key, shape, width, limit, shards=(), kind=jnp.bfloat16):
    gain = block_scale(stream_key, shape, shards, -0.22, 0.18) if shards else 1.0
    drawn = jax.random.normal(stream_key, shape, jnp.float32) * width * gain
    return jnp.minimum(jnp.maximum(drawn, -limit), limit).astype(kind)


def setup_inputs(seed: int = 0) -> dict:
    key_list = jax.random.split(jax.random.key(seed), 11)
    queries = draw_queries(jax.random.fold_in(key_list[10], 71), 0)
    keys = draw_keys(jax.random.fold_in(key_list[10], 71), 0)
    values = noise(key_list[2], (TOKENS, KV_HEADS * HD), 3.0, 16.0, ((0, 64), (1, 2)))
    offsets = draw_offsets(jax.random.fold_in(key_list[10], 71), 0)
    out_weight = noise(key_list[4], (HEADS * HD, D), (HEADS * HD) ** -0.5, 0.125, ((0, 2),))
    stream_in = draw_stream_in(jax.random.fold_in(key_list[10], 71), 0)
    norm_gain = jnp.clip(1.0 + 0.18 * jax.random.normal(key_list[6], (D,), jnp.float32), 0.1, 1.9)
    head_weight = draw_head_weight(jax.random.fold_in(key_list[10], 71), 0)
    picks = plant(jax.random.randint(key_list[8], (BATCH * SCORED,), 0, TOK_DEV), jax.random.fold_in(key_list[8], 1), 0, TOK_DEV - 1).astype(jnp.int32)
    targets = plant(jax.random.randint(key_list[9], (BATCH * SCORED,), 0, VOCAB), jax.random.fold_in(key_list[9], 1), 0, VOCAB - 1).astype(jnp.int32)
    return {"queries": queries, "keys": keys, "values": values, "offsets": offsets, "out_weight": out_weight, "stream_in": stream_in, "norm_gain": norm_gain, "head_weight": head_weight, "picks": picks, "targets": targets}


def reference(queries, keys, values, offsets, out_weight, stream_in, norm_gain, head_weight, picks, targets):
    scale = 1.0 / math.sqrt(HD)
    window = MAXLEN + QB
    key_pad = jnp.pad(keys.reshape(BATCH, PACK, KV_HEADS * HD), ((0, 0), (MAXLEN, 0), (0, 0)))
    value_pad = jnp.pad(values.reshape(BATCH, PACK, KV_HEADS * HD), ((0, 0), (MAXLEN, 0), (0, 0)))
    block_count = TOKENS // QB

    def attend(item):
        block = item // KV_HEADS
        group = item % KV_HEADS
        first = block * QB
        pack = first // PACK
        inner = first % PACK
        q_part = lax.dynamic_slice(queries, (first, group * GROUP * HD), (QB, GROUP * HD))
        q_part = q_part.reshape(QB, GROUP, HD).astype(jnp.float32)
        k_part = lax.dynamic_slice(key_pad, (pack, inner, group * HD), (1, window, HD))[0].astype(jnp.float32)
        v_part = lax.dynamic_slice(value_pad, (pack, inner, group * HD), (1, window, HD))[0].astype(jnp.float32)
        scores = jnp.einsum('qha,ka->hqk', q_part, k_part) * scale
        query_pos = inner + jnp.arange(QB, dtype=jnp.int32)
        key_pos = inner - MAXLEN + jnp.arange(window, dtype=jnp.int32)
        starts = lax.dynamic_slice_in_dim(offsets, first, QB)
        allowed = (key_pos[None, :] >= starts[:, None]) & (key_pos[None, :] <= query_pos[:, None])
        scores = jnp.where(allowed[None], scores, -jnp.inf)
        top = lax.optimization_barrier(jnp.max(scores, axis=-1, keepdims=True))
        weights = jnp.exp(scores - top)
        probs = (weights / lax.optimization_barrier(jnp.sum(weights, axis=-1, keepdims=True))).astype(jnp.bfloat16)
        mixed = jnp.einsum('hqk,ka->qha', probs.astype(jnp.float32), v_part)
        return mixed.astype(jnp.bfloat16).reshape(QB, GROUP * HD)
    pieces = lax.map(attend, jnp.arange(block_count * KV_HEADS, dtype=jnp.int32))
    context = pieces.reshape(block_count, KV_HEADS, QB, GROUP * HD).transpose(0, 2, 1, 3).reshape(TOKENS, HEADS * HD)
    half_width = HEADS * HD // 2
    branch = jnp.zeros((TOKENS, D), jnp.float32)
    for half in range(2):
        term = jnp.dot(context[:, half * half_width:(half + 1) * half_width], out_weight[half * half_width:(half + 1) * half_width], preferred_element_type=jnp.float32)
        term = lax.optimization_barrier(term.astype(jnp.bfloat16))
        branch = branch + term.astype(jnp.float32)
    stream_out = (stream_in.astype(jnp.float32) + branch).astype(jnp.bfloat16)
    order = jnp.arange(BATCH * SCORED, dtype=jnp.int32)
    rows = order // SC_DEV * TOK_DEV + picks
    chosen = stream_out[rows].astype(jnp.float32)
    inverse = lax.rsqrt(lax.optimization_barrier(jnp.mean(chosen * chosen, axis=-1, keepdims=True)) + 1e-05)
    normed = (chosen * inverse * norm_gain).astype(jnp.bfloat16)
    logits = lax.dot_general(normed, head_weight, (((1,), (1,)), ((), ())), preferred_element_type=jnp.float32)
    top = lax.optimization_barrier(jnp.max(logits, axis=-1))
    total = lax.optimization_barrier(jnp.sum(jnp.exp(logits - top[:, None]), axis=-1))
    target_logit = jnp.take_along_axis(logits, targets[:, None], axis=1)[:, 0]
    logprob = target_logit - top - jnp.log(total)
    return (stream_out, logprob)
```

```python
import functools
import math

import jax
import jax.numpy as jnp
from jax import lax
from jax.experimental import pallas as pl
from jax.experimental.pallas import tpu as pltpu
from jax.sharding import PartitionSpec as P

HD = 128
GROUP = 4
PIECES = 9
NEG = -1e30
ALL = ("dp", "seq", "mp")


def bar(*xs):
    return lax.optimization_barrier(xs)


def attend_kernel(tq, tiles, blk, info, pos_ref, off_ref, q_ref, *refs):
    k_refs, v_refs = refs[:PIECES], refs[PIECES : 2 * PIECES]
    o_ref, s_ref, mx_ref, sum_ref, acc_ref = refs[2 * PIECES :]
    gain = math.log2(math.e) / math.sqrt(HD)

    def tile(t, carry):
        first = pl.multiple_of(t * tq, tq)
        rows = pl.ds(first, tq)
        q4 = jnp.concatenate([q_ref[rows, h * HD : (h + 1) * HD] for h in range(GROUP)], axis=0)
        mx_ref[...] = jnp.full_like(mx_ref, NEG)
        for j in range(PIECES):
            mode = info[PIECES + t * PIECES + j]

            def put(masked, j=j):
                s = lax.dot_general(
                    q4, k_refs[j][...], (((1,), (1,)), ((), ())), preferred_element_type=jnp.float32
                )
                if masked:
                    at = info[j] + lax.broadcasted_iota(jnp.int32, (tq, blk), 1)
                    seen = (at >= off_ref[rows, :]) & (at <= pos_ref[rows, :])
                    s = jnp.concatenate(
                        [
                            jnp.where(seen, s[h * tq : (h + 1) * tq], NEG)
                            for h in range(GROUP)
                        ],
                        axis=0,
                    )
                s_ref[:, j * blk : (j + 1) * blk] = s
                top = s[:, :HD]
                for c in range(1, blk // HD):
                    top = jnp.maximum(top, s[:, c * HD : (c + 1) * HD])
                mx_ref[...] = jnp.maximum(mx_ref[...], top)

            pl.when(mode == 1)(functools.partial(put, False))
            pl.when(mode == 2)(functools.partial(put, True))
        top = jnp.max(mx_ref[...], axis=-1, keepdims=True)
        mx_ref[...] = jnp.broadcast_to(top, mx_ref.shape)
        sum_ref[...] = jnp.zeros_like(sum_ref)
        acc_ref[...] = jnp.zeros_like(acc_ref)
        for j in range(PIECES):
            mode = info[PIECES + t * PIECES + j]

            @pl.when(mode != 0)
            def _(j=j):
                m = mx_ref[...]
                parts = [
                    jnp.exp2((s_ref[:, j * blk + c * HD : j * blk + (c + 1) * HD] - m) * gain)
                    for c in range(blk // HD)
                ]
                add = parts[0]
                for p in parts[1:]:
                    add = add + p
                sum_ref[...] += add
                w = jnp.concatenate([p.astype(jnp.bfloat16) for p in parts], axis=1)
                acc_ref[...] += jnp.dot(w, v_refs[j][...], preferred_element_type=jnp.float32)

        total = jnp.sum(sum_ref[...], axis=-1, keepdims=True)
        out = (acc_ref[...] / total).astype(jnp.bfloat16)
        for h in range(GROUP):
            o_ref[rows, h * HD : (h + 1) * HD] = out[h * tq : (h + 1) * tq]
        return carry

    lax.fori_loop(0, tiles, tile, 0)


def attend(tq, group_first, group_count, info, pos, off, q, pieces):
    n = q.shape[0]
    blk = pieces[0].shape[0]
    groups = pieces[0].shape[1] // (2 * HD)
    whole = lambda g, *_: (0, 0)
    k_spec = pl.BlockSpec((blk, HD), lambda g, *_: (0, group_first + g))
    v_spec = pl.BlockSpec((blk, HD), lambda g, *_: (0, groups + group_first + g))
    rows4 = GROUP * tq
    return pl.pallas_call(
        functools.partial(attend_kernel, tq, n // tq, blk),
        out_shape=jax.ShapeDtypeStruct((n, group_count * GROUP * HD), jnp.bfloat16),
        grid_spec=pltpu.PrefetchScalarGridSpec(
            num_scalar_prefetch=1,
            grid=(group_count,),
            in_specs=[
                pl.BlockSpec((n, 1), whole),
                pl.BlockSpec((n, 1), whole),
                pl.BlockSpec((n, GROUP * HD), lambda g, *_: (0, group_first + g)),
            ]
            + [k_spec] * PIECES
            + [v_spec] * PIECES,
            out_specs=pl.BlockSpec((n, GROUP * HD), lambda g, *_: (0, g)),
            scratch_shapes=[
                pltpu.VMEM((rows4, PIECES * blk), jnp.float32),
                pltpu.VMEM((rows4, HD), jnp.float32),
                pltpu.VMEM((rows4, HD), jnp.float32),
                pltpu.VMEM((rows4, HD), jnp.float32),
            ],
        ),
        cost_estimate=pl.CostEstimate(
            flops=4 * n * group_count * GROUP * PIECES * blk * HD,
            transcendentals=n * group_count * GROUP * PIECES * blk,
            bytes_accessed=group_count * (PIECES * blk * 2 + n * 8) * HD * 2,
        ),
    )(info, pos, off, q, *pieces, *pieces)


def logits_kernel(steps, info, tgt_ref, x0, x1, x2, x3, w_ref, o_ref, l_ref):
    i = pl.program_id(0)
    vt = w_ref.shape[0]
    x = jnp.concatenate([r[...] for r in (x0, x1, x2, x3)], axis=0)
    l_ref[i] = lax.dot_general(
        x, w_ref[...], (((1,), (1,)), ((), ())), preferred_element_type=jnp.float32
    )

    @pl.when(i == steps - 1)
    def _():
        n = x.shape[0]
        top = l_ref[0]
        for k in range(1, steps):
            top = jnp.maximum(top, l_ref[k])
        top = jnp.max(top, axis=-1, keepdims=True)
        total = jnp.zeros((n, vt), jnp.float32)
        hit = jnp.zeros((n, vt), jnp.float32)
        for k in range(steps):
            lk = l_ref[k]
            total = total + jnp.exp(lk - top)
            col = info[k] + lax.broadcasted_iota(jnp.int32, (n, vt), 1)
            hit = hit + jnp.where(col == tgt_ref[...], lk, 0.0)
        total = jnp.sum(total, axis=-1, keepdims=True)
        hit = jnp.sum(hit, axis=-1, keepdims=True)
        lane = lax.broadcasted_iota(jnp.int32, (n, HD), 1)
        packed = jnp.where(lane == 0, top, jnp.where(lane == 1, total, hit))
        for b in range(n // 8):
            o_ref[info[steps + b]] = packed[b * 8 : b * 8 + 8]


def score_rows(info, tgt, xs, w):
    steps = 4
    n = 4 * xs[0].shape[0]
    d = w.shape[1]
    vt = w.shape[0] // steps
    return pl.pallas_call(
        functools.partial(logits_kernel, steps),
        out_shape=jax.ShapeDtypeStruct((n // 8, 8, HD), jnp.float32),
        grid_spec=pltpu.PrefetchScalarGridSpec(
            num_scalar_prefetch=1,
            grid=(steps,),
            in_specs=[pl.BlockSpec((n, 1), lambda i, *_: (0, 0))]
            + [pl.BlockSpec((n // 4, d), lambda i, *_: (0, 0))] * 4
            + [pl.BlockSpec((vt, d), lambda i, *_: (i, 0))],
            out_specs=pl.BlockSpec((n // 8, 8, HD), lambda i, *_: (0, 0, 0)),
            scratch_shapes=[pltpu.VMEM((steps, n, vt), jnp.float32)],
        ),
        cost_estimate=pl.CostEstimate(
            flops=2 * n * d * w.shape[0],
            transcendentals=n * w.shape[0],
            bytes_accessed=2 * d * (n + w.shape[0]),
        ),
    )(info, tgt, *xs, w)


def close_kernel(x_ref, o_ref):
    x = x_ref[...]
    top = jnp.max(x, axis=0)
    total = jnp.sum(pltpu.roll(x, HD - 1, 2) * jnp.exp(x - top[None]), axis=0)
    hit = jnp.sum(pltpu.roll(x, HD - 2, 2), axis=0)
    o_ref[...] = hit - top - jnp.log(total)


def gather_moves(stage):
    order = {0: "zyx", 1: "xzy"}

    def moved(x, y, z, axis, k):
        at = {"x": x, "y": y, "z": z}
        at[axis] = (at[axis] + k) % 4
        return at["x"], at["y"], at["z"]

    tables = []
    for k in (1, 2, 3):
        table = []
        for x in range(4):
            for y in range(4):
                for z in range(4):
                    for c in range(2):
                        a, b, d = moved(x, y, z, order[c][stage], k)
                        table.append((((x * 16 + y * 4 + z) * 2 + c), ((a * 16 + b * 4 + d) * 2 + c)))
        tables.append(table)
    return tables


def spread(x, stage):
    return [x] + [lax.ppermute(x, ALL, table) for table in gather_moves(stage)]


def on_device(
    queries, keys, values, offsets, out_weight, stream_in, norm_gain, head_weight, picks, targets
):
    rows = queries.shape[0]
    swap = [(0, 1), (1, 0)]
    seq_count = lax.axis_size("seq")
    seq = lax.axis_index("seq")
    dp = lax.axis_index("dp")
    core = lax.axis_index("mp")
    base = seq * rows
    kv = jnp.concatenate([keys, values], axis=1)
    pieces = [kv] + [
        lax.ppermute(kv, "seq", [(s, s + k) for s in range(seq_count - k)])
        for k in range(1, PIECES)
    ]
    other_weight = lax.ppermute(head_weight, "mp", swap)
    head = jnp.concatenate([head_weight, other_weight], axis=0)
    n_sc = picks.shape[0]
    own_sc = n_sc // 2

    q_sc = jnp.take(queries, picks, axis=0)
    pos_sc = (base + picks)[:, None]
    off_sc = jnp.take(offsets, picks, axis=0)[:, None]
    at = base - rows * jnp.arange(PIECES, dtype=jnp.int32)
    live = at >= 0
    info_sc = jnp.concatenate([at, jnp.where(live, 2, 0).astype(jnp.int32)])
    in_sc = jnp.take(stream_in, picks, axis=0)
    in_mine = lax.dynamic_slice_in_dim(in_sc, core * own_sc, own_sc)
    in_away = lax.ppermute(
        lax.dynamic_slice_in_dim(in_sc, (1 - core) * own_sc, own_sc), "mp", swap
    )
    in_rows = jnp.where(
        core == 0,
        jnp.concatenate([in_mine, in_away], axis=1),
        jnp.concatenate([in_away, in_mine], axis=1),
    ).astype(jnp.float32)

    ctx_sc = attend(n_sc, 0, 2, info_sc, pos_sc, off_sc, q_sc, pieces)
    part_sc = jnp.dot(ctx_sc, out_weight, preferred_element_type=jnp.float32).astype(jnp.bfloat16)
    part_mine = lax.dynamic_slice_in_dim(part_sc, core * own_sc, own_sc)
    part_away = lax.ppermute(
        lax.dynamic_slice_in_dim(part_sc, (1 - core) * own_sc, own_sc), "mp", swap
    )
    chosen = in_rows + (part_mine.astype(jnp.float32) + part_away.astype(jnp.float32))
    chosen = chosen.astype(jnp.bfloat16).astype(jnp.float32)
    inverse = lax.rsqrt(jnp.mean(chosen * chosen, axis=-1, keepdims=True) + 1e-05)
    normed = (chosen * inverse * norm_gain).astype(jnp.bfloat16)

    pos = (base + jnp.arange(rows, dtype=jnp.int32))[:, None]
    off = offsets[:, None]
    tq = 128
    tiles = rows // tq
    low = jnp.min(offsets.reshape(tiles, tq), axis=1)[:, None]
    high = jnp.max(offsets.reshape(tiles, tq), axis=1)[:, None]
    none = (at[None] + (rows - 1) < low) | ~live[None]
    every = (at[None] >= high) & (jnp.arange(PIECES)[None] > 0)
    modes = jnp.where(none, 0, jnp.where(every, 1, 2)).astype(jnp.int32)
    info = jnp.concatenate([at, modes.reshape(-1)])

    q0, normed = bar(queries, normed)
    stage_a = spread(normed, 0)
    ctx0 = attend(tq, 0, 1, info, pos, off, q0, pieces)
    block_a = jnp.concatenate(stage_a, axis=0)
    q1, block_a, ctx0 = bar(queries, block_a, ctx0)
    stage_b = spread(block_a, 1)
    ctx1 = attend(tq, 1, 1, info, pos, off, q1, pieces)
    block_b = jnp.concatenate(stage_b, axis=0)
    block_b, ctx1 = bar(block_b, ctx1)
    stage_c = spread(block_b, 2)
    ctx = jnp.concatenate([ctx0, ctx1], axis=1)
    part = jnp.dot(ctx, out_weight, preferred_element_type=jnp.float32).astype(jnp.bfloat16)
    half = stream_in.shape[1]
    mine = lax.dynamic_slice_in_dim(part, core * half, half, axis=1)
    away = lax.ppermute(
        lax.dynamic_slice_in_dim(part, (1 - core) * half, half, axis=1), "mp", swap
    )
    branch = mine.astype(jnp.float32) + away.astype(jnp.float32)
    stream_out = (stream_in.astype(jnp.float32) + branch).astype(jnp.bfloat16)

    step = jnp.arange(4, dtype=jnp.int32)
    c_at, b_at, a_at = step[:, None, None], step[None, :, None], step[None, None, :]
    y, z = seq // 4, seq % 4
    src0 = ((dp - c_at) % 4) * 16 + ((y - b_at) % 4) * 4 + (z - a_at) % 4
    src1 = ((dp - a_at) % 4) * 16 + ((y - c_at) % 4) * 4 + (z - b_at) % 4
    source = jnp.where(core == 0, src0, src1).reshape(-1)
    tgt = jnp.take(targets.reshape(-1, own_sc), source * 2 + core, axis=0).reshape(-1, 1)
    vocab_rows = head_weight.shape[0]
    flat = (dp * seq_count + seq) * 2 + core
    first = jnp.stack([flat, flat, flat ^ 1, flat ^ 1]) * vocab_rows
    first = first + jnp.array([0, vocab_rows // 2, 0, vocab_rows // 2], jnp.int32)
    info_lg = jnp.concatenate([first.astype(jnp.int32), source.astype(jnp.int32)])
    stats = score_rows(info_lg, tgt, stage_c, head)
    stats = lax.all_to_all(stats, ("dp", "seq"), 0, 0, tiled=True)
    logprob = pl.pallas_call(
        close_kernel, out_shape=jax.ShapeDtypeStruct((own_sc, HD), jnp.float32)
    )(stats)[:, 0]
    return (stream_out, logprob)


def solution(mesh):
    placed = (
        P(("dp", "seq"), "mp"),
        P(("dp", "seq"), "mp"),
        P(("dp", "seq"), "mp"),
        P(("dp", "seq")),
        P("mp", None),
        P(("dp", "seq"), "mp"),
        P(),
        P(("dp", "seq", "mp"), None),
        P(("dp", "seq")),
        P(),
    )
    return jax.shard_map(
        on_device,
        mesh=mesh,
        in_specs=placed,
        out_specs=(P(("dp", "seq"), "mp"), P(("dp", "seq", "mp"))),
        check_vma=False,
    )
```
